32 devices in a mesh: src: 8 (over z, y), rcv: 4 (over x, core).
Axes of the slice: x: 2, y: 2, z: 4, core: 2. Of those that a mesh axis runs over, the one named last changes fastest.
Arguments:
- src_traces: bfloat16 [2, 4, 256, 2048], P(None, 'rcv', 'src'), may hold values from -6 to 6
- rcv_traces: bfloat16 [2, 8, 512, 2048], P(None, 'src', 'rcv'), may hold values from -6 to 6
- src_owner: int32 [2, 8], P(None, 'src'), may hold values from 0 to 3
- rcv_owner: int32 [2, 4], P(None, 'rcv'), may hold values from 0 to 7
- active: int32 [8, 16], P('src', 'rcv'), may hold values 0 or 1
Outputs:
- stacked: float32 [256, 512, 128], P('src', 'rcv')
The draws below stay inside these ranges and needn't reach their ends.
Inputs may be any that keep to these rules, and one draw needn't show every extreme that they name: src_owner names a slot of the rcv dimension. rcv_owner names a slot of the src dimension.
All inputs are finite; a program needn't handle non-finite values. No bound on the sum of `active` on one device may be relied on, other than what follows from the above.
Results may differ from the reference program's by a relative error of at most 0.004.
Values may be sent and summed in bfloat16 or wider, within the bound.
No kernel may reach another device: no remote copies, remote signals or barrier semaphores. Data moves between devices by JAX's collectives and lax.ppermute only.
A program may use at most 128 MiB of HBM per device.

```python
import jax
import jax.numpy as jnp
from jax import lax

SRC_DEV = 32
RCV_DEV = 128
SAMPLES = 2048
LAGS = 128
BLOCK = 32
WINDOWS = 2
SOURCES = 256
RECEIVERS = 512
N_SRC = 8
N_RCV = 4


def plant(array, key, smallest, high):
    dims = array.shape
    place = [jax.random.randint(jax.random.fold_in(key, axis), (), 0, dims[axis]) for axis in range(len(dims))]
    array = array.at[tuple(place)].set(smallest)
    longest = dims.index(max(dims))
    place[longest] = (place[longest] + 1) % dims[longest]
    return array.at[tuple(place)].set(high)


def steps_of(stream_key, shape, split, low, largest):
    gain, own = 1.0, jax.random.fold_in(stream_key, 6)
    for dim, parts in split:
        draws = jnp.exp(jax.random.uniform(jax.random.fold_in(own, dim), (parts,), jnp.float32, low / len(split), largest / len(split)))
        gain = gain * jnp.repeat(draws, shape[dim] // parts).reshape([-1 if axis == dim else 1 for axis in range(len(shape))])
    return gain


def noise(key, extent, width, most, shards=(), kind=jnp.bfloat16):
    result = jax.random.normal(key, extent, jnp.float32) * width
    if len(shards) > 0:
        result = steps_of(key, extent, shards, -0.22, 0.18) * result
    return jnp.clip(result, min=-most, max=most).astype(kind)


def setup_inputs(seed: int = 0) -> dict:
    streams_of = jax.random.split(jax.random.key(seed), 6)
    src_traces = noise(streams_of[0], (WINDOWS, N_RCV, SOURCES, SAMPLES), 1.0, 6.0, ((1, 4), (2, 8)))
    rcv_traces = noise(streams_of[1], (WINDOWS, N_SRC, RECEIVERS, SAMPLES), 1.0, 6.0, ((1, 8), (2, 4)))
    src_owner = plant(jax.random.randint(streams_of[2], (WINDOWS, N_SRC), 0, N_RCV), jax.random.fold_in(streams_of[2], 1), 0, N_RCV - 1).astype(jnp.int32)
    rcv_owner = plant(jax.random.randint(streams_of[3], (WINDOWS, N_RCV), 0, N_SRC), jax.random.fold_in(streams_of[3], 1), 0, N_SRC - 1).astype(jnp.int32)
    active = plant((jax.random.randint(streams_of[4], (SOURCES // BLOCK, RECEIVERS // BLOCK), 0, 2) < 1).astype(jnp.int32), jax.random.fold_in(streams_of[4], 1), 0, 1)
    return {"src_traces": src_traces, "rcv_traces": rcv_traces, "src_owner": src_owner, "rcv_owner": rcv_owner, "active": active}


epsilon = 1e-06

def normalise(traces):
    values = traces.astype(jnp.float32)
    energy = lax.optimization_barrier(jnp.mean(values * values, axis=-1, keepdims=True))
    return (values * lax.rsqrt(energy + epsilon)).astype(jnp.bfloat16)

def reference(src_traces, rcv_traces, src_owner, rcv_owner, active):
    src_chan = jnp.arange(SOURCES, dtype=jnp.int32)
    rcv_chan = jnp.arange(RECEIVERS, dtype=jnp.int32)
    src_group = src_chan // SRC_DEV
    rcv_group = rcv_chan // RCV_DEV
    span = SAMPLES - LAGS
    totals = jnp.zeros((SOURCES, RECEIVERS, LAGS), jnp.float32)
    for window in range(WINDOWS):
        first = normalise(src_traces[window, src_owner[window][src_group], src_chan]).astype(jnp.float32)
        second = normalise(rcv_traces[window, rcv_owner[window][rcv_group], rcv_chan]).astype(jnp.float32)
        leading = first[:, :span]

        def one_lag(shift):
            moved = lax.dynamic_slice_in_dim(second, shift, span, 1)
            return jnp.dot(leading, moved.T, precision=lax.Precision.HIGHEST, preferred_element_type=jnp.float32)
        per_lag = lax.map(one_lag, jnp.arange(LAGS, dtype=jnp.int32))
        totals = totals + jnp.transpose(per_lag, (1, 2, 0))
    listed = jnp.repeat(jnp.repeat(active, BLOCK, axis=0), BLOCK, axis=1).astype(jnp.float32)
    scale = 1.0 / jnp.sqrt(jnp.float32(span * WINDOWS))
    return totals * listed[:, :, None] * scale
```

```python
import functools

import jax
import jax.numpy as jnp
from jax import lax
from jax.experimental import pallas as pl
from jax.experimental.pallas import tpu as pltpu
from jax.sharding import PartitionSpec as P

LAGS = 128
BLOCK = 32
LOW = 16
COLS = 256


epsilon = 1e-06

VM = pl.BlockSpec(memory_space=pltpu.VMEM)
SM = pl.BlockSpec(memory_space=pltpu.SMEM)


def unit(values):
    energy = jnp.mean(values * values, axis=-1, keepdims=True)
    return values * lax.rsqrt(energy + epsilon)


def split_kernel(deep, wide, raw_ref, *sets):
    windows, _, samples = raw_ref.shape
    seg = samples // (deep * wide)
    for window in range(windows):
        flat = unit(raw_ref[window].astype(jnp.float32)).astype(jnp.bfloat16)
        turned = flat.T
        for a in range(deep):
            for b in range(wide):
                q = a * wide + b
                sets[window * wide + b][a] = turned[q * seg : (q + 1) * seg]


def toeplitz_kernel(rel_ref, *refs):
    slots, out_ref = refs[:-2], refs[-2]
    held = refs[-1]
    windows, count, samples = held.shape
    span = samples - LAGS
    for window in range(windows):
        for slot, ref in enumerate(slots):

            @pl.when(rel_ref[window] == slot)
            def _(ref=ref, window=window):
                held[window] = ref[window]

        rows = unit(held[window].astype(jnp.float32)).astype(jnp.bfloat16).astype(jnp.float32)
        lane = lax.broadcasted_iota(jnp.int32, rows.shape, 1)
        rows = jnp.where(lane < span, rows, 0.0)
        for s in range(count):
            line = jnp.broadcast_to(rows[s : s + 1], (8, samples))
            parts = [pltpu.roll(line, j, 1, stride=1, stride_axis=0) for j in range(0, LOW, 8)]
            out_ref[window, s * LOW : (s + 1) * LOW, :] = jnp.concatenate(parts, axis=0).astype(jnp.bfloat16)


def place(rel_ref, window, groups, turned, wide):
    deep, seg, count = groups[0].shape
    samples = deep * wide * seg
    for b, group in enumerate(groups):
        for a in range(deep):
            at = jnp.bitwise_xor(rel_ref[window], a * wide + b)
            turned[pl.ds(pl.multiple_of(at * seg, seg), seg), :] = group[a]
    turned[samples:, :] = jnp.zeros((LAGS, count), jnp.bfloat16)


def product(left, turned, samples, high):
    moved = [turned[h * LOW : h * LOW + samples, :] for h in high]
    return jnp.dot(left, jnp.concatenate(moved, axis=1), preferred_element_type=jnp.float32)


def first_kernel(wide, rel_ref, left_ref, *refs):
    groups, acc_ref, turned = refs[:wide], refs[wide], refs[wide + 1]
    samples, count = left_ref.shape[1], turned.shape[1]
    place(rel_ref, 0, groups, turned, wide)
    pair = COLS // count
    for j in range(LAGS // LOW // pair):
        acc_ref[:, j * COLS : (j + 1) * COLS] = product(
            left_ref[...], turned, samples, range(j * pair, (j + 1) * pair)
        )


def last_kernel(wide, scale, rel_ref, active_ref, left_ref, acc_ref, *refs):
    groups, out_ref, turned, total = refs[:wide], refs[wide], refs[wide + 1], refs[wide + 2]
    samples, count = left_ref.shape[1], turned.shape[1]
    place(rel_ref, 1, groups, turned, wide)
    pair = COLS // count
    for j in range(LAGS // LOW // pair):
        cut = slice(j * COLS, (j + 1) * COLS)
        total[:, cut] = acc_ref[:, cut] + product(
            left_ref[...], turned, samples, range(j * pair, (j + 1) * pair)
        )
    row = lax.broadcasted_iota(jnp.int32, (count, 1), 0)
    weight = jnp.zeros((count, 1), jnp.float32)
    for block in range(count // BLOCK):
        flag = active_ref[0, block].astype(jnp.float32)
        weight = jnp.where(row // BLOCK == block, flag, weight)
    for s in range(out_ref.shape[0]):
        rows = total[s * LOW : (s + 1) * LOW, :]
        lags = jnp.concatenate([rows[:, h * count : (h + 1) * count] for h in range(LAGS // LOW)], axis=0)
        out_ref[s] = lags.T * weight * scale


def pick(index, choices):
    result = choices[0]
    for i, choice in enumerate(choices[1:], 1):
        result = jnp.where(index == i, choice, result)
    return result


def swap(value, axis, size, gap):
    return lax.ppermute(value, axis, [(i, i ^ gap) for i in range(size)])


def body(n_src, n_rcv, src_traces, rcv_traces, src_owner, rcv_owner, active):
    windows, _, src_count, samples = src_traces.shape
    rcv_count = rcv_traces.shape[2]
    wide = 1
    while 4 * wide * wide <= n_src:
        wide *= 2
    deep = n_src // wide
    seg = samples // n_src
    src_rel = jnp.bitwise_xor(src_owner[:, 0], lax.axis_index("rcv"))
    rcv_rel = jnp.bitwise_xor(rcv_owner[:, 0], lax.axis_index("src"))

    own = src_traces[:, 0]
    slots = [own] + [swap(own, "rcv", n_rcv, gap) for gap in range(1, n_rcv)]

    sets = pl.pallas_call(
        functools.partial(split_kernel, deep, wide),
        out_shape=[jax.ShapeDtypeStruct((deep, seg, rcv_count), jnp.bfloat16)] * (windows * wide),
        in_specs=[VM],
        out_specs=[VM] * (windows * wide),
    )(rcv_traces[:, 0])

    gathered = []
    for window in range(windows):
        mine = sets[window * wide : (window + 1) * wide]
        rel_wide, rel_deep = rcv_rel[window] % wide, rcv_rel[window] // wide
        arrived = [mine[0]] + [swap(mine[b], "src", n_src, b) for b in range(1, wide)]
        rows = pick(rel_wide, arrived)
        arrived = [rows[0]] + [swap(rows[a], "src", n_src, a * wide) for a in range(1, deep)]
        piece = pick(rel_deep, arrived)
        group = jnp.stack([piece] + [swap(piece, "src", n_src, a * wide) for a in range(1, deep)])
        gathered.append([group] + [swap(group, "src", n_src, b) for b in range(1, wide)])

    left = pl.pallas_call(
        toeplitz_kernel,
        out_shape=jax.ShapeDtypeStruct((windows, src_count * LOW, samples), jnp.bfloat16),
        in_specs=[SM] + [VM] * n_rcv,
        out_specs=VM,
        scratch_shapes=[pltpu.VMEM((windows, src_count, samples), jnp.bfloat16)],
    )(src_rel, *slots)

    turned = pltpu.VMEM((samples + LAGS, rcv_count), jnp.bfloat16)
    total = jax.ShapeDtypeStruct((src_count * LOW, LAGS // LOW * rcv_count), jnp.float32)
    acc = pl.pallas_call(
        functools.partial(first_kernel, wide),
        out_shape=total,
        in_specs=[SM, VM] + [VM] * wide,
        out_specs=VM,
        scratch_shapes=[turned],
    )(rcv_rel, left[0], *gathered[0])
    scale = 1.0 / float((samples - LAGS) * windows) ** 0.5
    return pl.pallas_call(
        functools.partial(last_kernel, wide, scale),
        out_shape=jax.ShapeDtypeStruct((src_count, rcv_count, LAGS), jnp.float32),
        in_specs=[SM, SM, VM, VM] + [VM] * wide,
        out_specs=VM,
        scratch_shapes=[turned, pltpu.VMEM(total.shape, jnp.float32)],
    )(rcv_rel, active, left[1], acc, *gathered[1])


def solution(mesh):
    return jax.shard_map(
        functools.partial(body, mesh.shape["src"], mesh.shape["rcv"]),
        mesh=mesh,
        in_specs=(
            P(None, "rcv", "src", None),
            P(None, "src", "rcv", None),
            P(None, "src"),
            P(None, "rcv"),
            P("src", "rcv"),
        ),
        out_specs=P("src", "rcv", None),
        check_vma=False,
    )
```

```python
import functools

import jax
import jax.numpy as jnp
from jax import lax
from jax.experimental import pallas as pl
from jax.experimental.pallas import tpu as pltpu
from jax.sharding import PartitionSpec as P

LAGS = 128
BLOCK = 32
LOW = 16
COLS = 256


epsilon = 1e-06

VM = pl.BlockSpec(memory_space=pltpu.VMEM)
SM = pl.BlockSpec(memory_space=pltpu.SMEM)


def limit(mib):
    return pltpu.CompilerParams(vmem_limit_bytes=mib << 20)


def unit(values):
    energy = jnp.mean(values * values, axis=-1, keepdims=True)
    return (values * lax.rsqrt(energy + epsilon)).astype(jnp.bfloat16)


def split_kernel(names, raw_ref, *refs):
    outs = refs[-len(names) :]
    turned = unit(raw_ref[0, 0].astype(jnp.float32)).T
    for qs, out in zip(names, outs):
        seg = out.shape[1]
        for i, q in enumerate(qs):
            out[i] = turned[q * seg : (q + 1) * seg]


def split_both_kernel(names, raw_ref, src_ref, *outs):
    split_kernel(names, raw_ref, *outs[1:])
    for window in range(src_ref.shape[0]):
        outs[0][window] = unit(src_ref[window, 0].astype(jnp.float32))


def pick_kernel(axis, window, shift, size, owner_ref, *refs):
    parts = refs[0].shape[0]
    choices, outs = refs[: len(refs) - parts], refs[len(refs) - parts :]
    rel = jnp.bitwise_xor(owner_ref[window, 0], lax.axis_index(axis))
    rel = jnp.bitwise_and(lax.shift_right_logical(rel, shift), size - 1)
    for i, choice in enumerate(choices):

        @pl.when(rel == i)
        def _(choice=choice):
            for part, out in enumerate(outs):
                out[0] = choice[part]


def toeplitz_kernel(windows, owner_ref, *refs):
    slots, outs, held = refs[: -1 - windows], refs[-1 - windows : -1], refs[-1]
    _, count, samples = held.shape
    span = samples - LAGS
    for window in range(windows):
        rel = jnp.bitwise_xor(owner_ref[window, 0], lax.axis_index("rcv"))
        for slot, ref in enumerate(slots):

            @pl.when(rel == slot)
            def _(ref=ref, window=window):
                held[window] = ref[window]

        rows = held[window].astype(jnp.float32)
        lane = lax.broadcasted_iota(jnp.int32, rows.shape, 1)
        rows = jnp.where(lane < span, rows, 0.0)
        for s in range(count):
            line = jnp.broadcast_to(rows[s : s + 1], (8, samples))
            parts = [pltpu.roll(line, j, 1, stride=1, stride_axis=0) for j in range(0, LOW, 8)]
            outs[window][s * LOW : (s + 1) * LOW, :] = jnp.concatenate(parts, axis=0).astype(jnp.bfloat16)


def place(rel, names, groups, turned):
    samples = turned.shape[0] - LAGS
    for qs, group in zip(names, groups):
        seg = group.shape[1]
        for i, q in enumerate(qs):
            at = jnp.bitwise_xor(rel, q)
            turned[pl.ds(pl.multiple_of(at * seg, seg), seg), :] = group[i]
    turned[samples:, :] = jnp.zeros((LAGS, turned.shape[1]), jnp.bfloat16)


def product(left, turned, samples, high):
    moved = [turned[h * LOW : h * LOW + samples, :] for h in high]
    return jnp.dot(left, jnp.concatenate(moved, axis=1), preferred_element_type=jnp.float32)


def first_kernel(names, owner_ref, left_ref, *refs):
    groups, (acc_ref, turned) = refs[: len(names)], refs[len(names) :]
    samples, count = left_ref.shape[1], turned.shape[1]
    rel = jnp.bitwise_xor(owner_ref[0, 0], lax.axis_index("src"))
    place(rel, names, groups, turned)
    pair = COLS // count
    for j in range(LAGS // LOW // pair):
        acc_ref[:, j * COLS : (j + 1) * COLS] = product(
            left_ref[...], turned, samples, range(j * pair, (j + 1) * pair)
        )


def last_kernel(names, scale, owner_ref, active_ref, left_ref, acc_ref, *refs):
    groups, (out_ref, turned, total) = refs[: len(names)], refs[len(names) :]
    samples, count = left_ref.shape[1], turned.shape[1]
    rel = jnp.bitwise_xor(owner_ref[1, 0], lax.axis_index("src"))
    place(rel, names, groups, turned)
    pair = COLS // count
    for j in range(LAGS // LOW // pair):
        cut = slice(j * COLS, (j + 1) * COLS)
        total[:, cut] = acc_ref[:, cut] + product(
            left_ref[...], turned, samples, range(j * pair, (j + 1) * pair)
        )
    row = lax.broadcasted_iota(jnp.int32, (count, 1), 0)
    weight = jnp.zeros((count, 1), jnp.float32)
    for block in range(count // BLOCK):
        flag = active_ref[0, block].astype(jnp.float32)
        weight = jnp.where(row // BLOCK == block, flag, weight)
    for s in range(out_ref.shape[0]):
        rows = total[s * LOW : (s + 1) * LOW, :]
        lags = jnp.concatenate([rows[:, h * count : (h + 1) * count] for h in range(LAGS // LOW)], axis=0)
        out_ref[s] = lags.T * weight * scale


def swap(value, axis, size, gap):
    return lax.ppermute(value, axis, [(i, i ^ gap) for i in range(size)])


def body(direct, n_src, n_rcv, src_traces, rcv_traces, src_owner, rcv_owner, active):
    windows, _, src_count, samples = src_traces.shape
    rcv_count = rcv_traces.shape[2]
    wide = 1
    while 4 * wide * wide <= n_src:
        wide *= 2
    deep = n_src // wide
    seg = samples // n_src

    def split(window, names, sources=None):
        shapes = [jax.ShapeDtypeStruct((len(qs), seg, rcv_count), jnp.bfloat16) for qs in names]
        specs = [pl.BlockSpec((1, 1, rcv_count, samples), lambda _: (window, 0, 0, 0))]
        args = [rcv_traces]
        kernel = split_kernel
        if sources is not None:
            shapes.insert(0, jax.ShapeDtypeStruct((windows, src_count, samples), jnp.bfloat16))
            specs.append(pl.BlockSpec(sources.shape, lambda _: (0, 0, 0, 0)))
            args.append(sources)
            kernel = split_both_kernel
        return pl.pallas_call(
            functools.partial(kernel, names),
            grid=(1,),
            out_shape=shapes,
            in_specs=specs,
            out_specs=[pl.BlockSpec(s.shape, lambda _: (0, 0, 0)) for s in shapes],
            compiler_params=limit(16),
        )(*args)

    def hop(value, gap):
        return swap(value, "src", n_src, gap)

    def pick(window, shift, size, choices):
        shape = jax.ShapeDtypeStruct((1,) + choices[0].shape[1:], choices[0].dtype)
        parts = choices[0].shape[0]
        return pl.pallas_call(
            functools.partial(pick_kernel, "src", window, shift, size),
            out_shape=[shape] * parts,
            in_specs=[SM] + [VM] * len(choices),
            out_specs=[VM] * parts,
            compiler_params=limit(8),
        )(rcv_owner, *choices)

    bits = wide.bit_length() - 1
    every = [[q] for q in range(n_src)]
    halves = [[a * wide + b for a in range(deep)] for b in range(wide)]
    sets, scattered = [], []
    for window in range(windows):
        names = every if window in direct else halves
        if window == 0:
            sets.append(split(window, names))
        else:
            sources, *rest = split(window, names, src_traces)
            sets.append(rest)
        scattered.append([sets[window][0]] + [hop(sets[window][i], i) for i in range(1, len(names))])
    slots = [sources] + [swap(sources, "rcv", n_rcv, gap) for gap in range(1, n_rcv)]

    gathered, names = [], []
    for window in range(windows):
        if window in direct:
            (piece,) = pick(window, 0, n_src, scattered[window])
        else:
            rows = pick(window, 0, wide, scattered[window])
            arrived = [rows[0]] + [hop(rows[a], a * wide) for a in range(1, deep)]
            (piece,) = pick(window, bits, deep, arrived)
        row = [piece] + [hop(piece, a * wide) for a in range(1, deep)]
        group = jnp.concatenate(row)
        gathered.append([group] + [hop(group, b) for b in range(1, wide)])
        names.append(halves)

    shape = jax.ShapeDtypeStruct((src_count * LOW, samples), jnp.bfloat16)
    left = pl.pallas_call(
        functools.partial(toeplitz_kernel, windows),
        out_shape=[shape] * windows,
        in_specs=[SM] + [VM] * n_rcv,
        out_specs=[VM] * windows,
        scratch_shapes=[pltpu.VMEM((windows, src_count, samples), jnp.bfloat16)],
        compiler_params=limit(20),
    )(src_owner, *slots)

    turned = pltpu.VMEM((samples + LAGS, rcv_count), jnp.bfloat16)
    total = jax.ShapeDtypeStruct((src_count * LOW, LAGS // LOW * rcv_count), jnp.float32)
    acc = pl.pallas_call(
        functools.partial(first_kernel, names[0]),
        out_shape=total,
        in_specs=[SM, VM] + [VM] * len(names[0]),
        out_specs=VM,
        scratch_shapes=[turned],
        compiler_params=limit(20),
    )(rcv_owner, left[0], *gathered[0])
    scale = 1.0 / float((samples - LAGS) * windows) ** 0.5
    return pl.pallas_call(
        functools.partial(last_kernel, names[1], scale),
        out_shape=jax.ShapeDtypeStruct((src_count, rcv_count, LAGS), jnp.float32),
        in_specs=[SM, SM, VM, VM] + [VM] * len(names[1]),
        out_specs=VM,
        scratch_shapes=[turned, pltpu.VMEM(total.shape, jnp.float32)],
        compiler_params=limit(24),
    )(rcv_owner, active, left[1], acc, *gathered[1])


DIRECT = ()


def solution(mesh):
    return jax.shard_map(
        functools.partial(body, DIRECT, mesh.shape["src"], mesh.shape["rcv"]),
        mesh=mesh,
        in_specs=(
            P(None, "rcv", "src", None),
            P(None, "src", "rcv", None),
            P(None, "src"),
            P(None, "rcv"),
            P("src", "rcv"),
        ),
        out_specs=P("src", "rcv", None),
        check_vma=False,
    )
```
